32 devices in a mesh: wide: 8 (over y, x, core), narrow: 4 (over z).
Axes of the slice: x: 2, y: 2, z: 4, core: 2. Of those that a mesh axis runs over, the one named last changes fastest.
Arguments:
- states: bfloat16 [16384, 1024], P(('wide', 'narrow')), may hold values from -6 to 6
- applied: bfloat16 [16384, 1024], P(('wide', 'narrow')), may hold values from -6 to 6
- rotation: bfloat16 [2, 1024, 256], P(None, 'wide', 'narrow'), may hold values from -0.1875 to 0.1875
- ritz: float32 [2, 256], replicated, may hold values from 0.5 to 4
- potential: float32 [16384], P(('wide', 'narrow')), may hold values from 0.5 to 8
Outputs:
- rotated: bfloat16 [16384, 2, 256], P(('wide', 'narrow'))
- correction: bfloat16 [16384, 2, 256], P(('wide', 'narrow'))
- margin: float32 [2, 1024, 256], P(None, 'wide', 'narrow')
The draws below stay inside these ranges and needn't reach their ends.
All inputs are finite; a program needn't handle non-finite values.
Results may differ from the reference program's by a relative error of at most 0.0095.
Values may be sent and summed in bfloat16 or wider, within the bound.
A program may use at most 64 MiB of HBM per device.

```python
import math
import jax
import jax.numpy as jnp

NST = 1024
BLOCK = 256
NBLOCKS = 2
ROWS = 16384


def strengthened(drawn, own_key, source, target, parts, factor):
    def block_of(axis_at):
        return (jnp.arange(drawn.shape[axis_at]) // (drawn.shape[axis_at] // parts)).reshape((-1,) + (1,) * (drawn.ndim - 1 - axis_at))

    one_side = jax.random.permutation(own_key, parts)[block_of(target)]
    other_side = (block_of(target) + parts // 2) % parts
    return jnp.where((block_of(source) == one_side) | (block_of(source) == other_side), factor * drawn, drawn)


def shard_levels(key, dims, pieces, smallest, high):
    def one(position, blocks):
        draws = jax.random.uniform(jax.random.fold_in(jax.random.fold_in(key, 6), position), (blocks,), jnp.float32, smallest / len(pieces), high / len(pieces))
        return jnp.repeat(jnp.exp(draws), dims[position] // blocks).reshape((-1,) + (1,) * (len(dims) - position - 1))

    loudness = one(*pieces[0])
    for cut in pieces[1:]:
        loudness = loudness * one(*cut)
    return loudness


def scatter_about(rng, extent, width, bound, pieces=(), dtype=jnp.bfloat16):
    entries = jax.random.normal(rng, extent, jnp.float32) * width
    if len(pieces) > 0:
        entries = shard_levels(rng, extent, pieces, -0.22, 0.18) * entries
    return jnp.clip(entries, min=-bound, max=bound).astype(dtype)


def gaussian_with(key, extent, scale, most, cuts, heavy, held_as=jnp.bfloat16):
    array = scale * jax.random.normal(key, extent, jnp.float32)
    if cuts:
        array = array * shard_levels(key, extent, cuts, -0.22, 0.18)
    return jnp.clip(strengthened(array, jax.random.fold_in(key, 3), *heavy), -most, most).astype(held_as)


def setup_inputs(seed: int = 0) -> dict:
    streams_of = jax.random.split(jax.random.key(seed), 6)
    states = gaussian_with(streams_of[0], (ROWS, NST), 1.0, 6.0, ((0, 32),), (0, 1, 32, 2.75))
    applied = scatter_about(streams_of[1], (ROWS, NST), 1.0, 6.0, ((0, 32),))
    rotation = scatter_about(streams_of[2], (NBLOCKS, NST, BLOCK), NST ** -0.5, 0.1875, ((1, 8), (2, 4)))
    ritz = jnp.clip(jax.random.uniform(streams_of[3], (NBLOCKS, BLOCK), jnp.float32, 0.5, 4.0), 0.5, 4.0)
    potential = jnp.clip(jnp.exp(math.log(8.0) - 2.7725887 * jax.random.uniform(streams_of[4], (ROWS,), jnp.float32) ** shard_levels(streams_of[4], (ROWS,), ((0, 32),), -0.2, 0.2)), 0.5, 8.0)
    return {"states": states, "applied": applied, "rotation": rotation, "ritz": ritz, "potential": potential}


def reference(states, applied, rotation, ritz, potential):
    factor = 1.0 / math.sqrt(ROWS)
    rotated_list = []
    correction_list = []
    margin_list = []
    for window in range(NBLOCKS):
        plain = jnp.dot(states, rotation[window], preferred_element_type=jnp.float32)
        mapped = jnp.dot(applied, rotation[window], preferred_element_type=jnp.float32)
        eigen_values = ritz[window]
        residual = mapped - plain * eigen_values[None, :]
        fixed = (residual / (potential[:, None] + eigen_values[None, :])).astype(jnp.bfloat16)
        summed = jnp.dot(states.T, fixed, preferred_element_type=jnp.float32)
        rotated_list.append(plain.astype(jnp.bfloat16))
        correction_list.append(fixed)
        margin_list.append(summed * factor)
    return (jnp.stack(rotated_list, axis=1), jnp.stack(correction_list, axis=1), jnp.stack(margin_list, axis=0))
```

```python
import functools
import math

import jax
import jax.numpy as jnp
from jax import lax
from jax.experimental import pallas as pl
from jax.experimental.pallas import tpu as pltpu
from jax.sharding import PartitionSpec as P

F32 = jnp.float32
BF16 = jnp.bfloat16
CORE, XBIT, YBIT = 1, 2, 4


def flip(index, mask):
    out = index
    bit = 1
    while bit <= mask:
        if mask & bit:
            out = out + bit * (1 - 2 * ((index // bit) % 2))
        bit *= 2
    return out


def fused_kernel(
    factor, narrow,
    q_ref, ritz_ref, pot_ref, x_hbm, hx_hbm,
    rot_ref, cor_ref, mar_ref,
    x, hx, g, inv, p32, p16, a16, r1, r2, r3, f32s, f16, r4,
    in_sem, zs, zr, gs, gr, ds, dr, cs, cr, s1, t1, s2, t2, s3, t3, s4, t4,
):
    w = lax.axis_index("wide")
    n = lax.axis_index("narrow")
    blocks = q_ref.shape[0]
    wide_to = lambda mask: {"wide": flip(w, mask)}
    narrow_to = lambda d: {"narrow": flip(n, d)}
    sends = []

    def push(src, dst, send, recv, to):
        copy = pltpu.make_async_remote_copy(
            src_ref=src, dst_ref=dst, send_sem=send, recv_sem=recv,
            device_id=to, device_id_type=pl.DeviceIdType.MESH)
        copy.start()
        sends.append(copy)

    def arrived(dst, send, recv, to):
        pltpu.make_async_remote_copy(
            src_ref=dst, dst_ref=dst, send_sem=send, recv_sem=recv,
            device_id=to, device_id_type=pl.DeviceIdType.MESH).wait_recv()

    load_x = pltpu.make_async_copy(x_hbm, x, in_sem.at[0])
    load_hx = pltpu.make_async_copy(hx_hbm, hx, in_sem.at[1])
    load_x.start()
    load_hx.start()

    barrier = pltpu.get_barrier_semaphore()
    peers = [wide_to(m) for m in (CORE, XBIT, YBIT)] + [narrow_to(d) for d in range(1, narrow)]
    for peer in peers:
        pl.semaphore_signal(barrier, inc=1, device_id=peer, device_id_type=pl.DeviceIdType.MESH)
    pl.semaphore_wait(barrier, len(peers))

    wc, wx, wy, wd = (flip(w, m) for m in (CORE, XBIT, YBIT, XBIT | YBIT))
    near = (XBIT, YBIT, CORE)
    for d in range(1, narrow):
        push(q_ref, g.at[w, :, n], zs.at[d], zr.at[d], narrow_to(d))
    for i, m in enumerate(near):
        push(q_ref, g.at[w, :, n], gs.at[i, 0], gr.at[i, 0], wide_to(m))
    g[w, :, n] = q_ref[...]
    for d in range(1, narrow):
        nd = flip(n, d)
        arrived(g.at[w, :, nd], zs.at[d], zr.at[d], narrow_to(d))
        for i, m in enumerate(near):
            push(g.at[w, :, nd], g.at[w, :, nd], gs.at[i, d], gr.at[i, d], wide_to(m))

    pot_col = jnp.transpose(jnp.broadcast_to(pot_ref[...], (128, pot_ref.shape[1])))[:, :1]
    for k in range(blocks):
        inv[k] = 1.0 / (pot_col + ritz_ref[k : k + 1, :])

    for d in range(narrow):
        nd = flip(n, d)
        arrived(g.at[wx, :, nd], gs.at[0, d], gr.at[0, d], wide_to(XBIT))
        push(g.at[wx, 1, nd], g.at[wx, 1, nd], ds.at[1, d], dr.at[1, d], wide_to(YBIT))
        push(g.at[wx, :, nd], g.at[wx, :, nd], cs.at[0, d], cr.at[0, d], wide_to(CORE))
        arrived(g.at[wy, :, nd], gs.at[1, d], gr.at[1, d], wide_to(YBIT))
        push(g.at[wy, 0, nd], g.at[wy, 0, nd], ds.at[0, d], dr.at[0, d], wide_to(XBIT))
        push(g.at[wy, :, nd], g.at[wy, :, nd], cs.at[1, d], cr.at[1, d], wide_to(CORE))
    for d in range(narrow):
        nd = flip(n, d)
        for k, m in ((0, XBIT), (1, YBIT)):
            arrived(g.at[wd, k, nd], ds.at[k, d], dr.at[k, d], wide_to(m))
            push(g.at[wd, k, nd], g.at[wd, k, nd], cs.at[2 + k, d], cr.at[2 + k, d], wide_to(CORE))
    for d in range(narrow):
        nd = flip(n, d)
        arrived(g.at[wc, :, nd], gs.at[2, d], gr.at[2, d], wide_to(CORE))
        arrived(g.at[flip(wx, CORE), :, nd], cs.at[0, d], cr.at[0, d], wide_to(CORE))
        arrived(g.at[flip(wy, CORE), :, nd], cs.at[1, d], cr.at[1, d], wide_to(CORE))
        for k in range(2):
            arrived(g.at[flip(wd, CORE), k, nd], cs.at[2 + k, d], cr.at[2 + k, d], wide_to(CORE))
    load_x.wait()
    load_hx.wait()

    wide = g.shape[0]
    cols = g.shape[2] * g.shape[3]
    depth = g.shape[4]
    last = (((1,), (1,)), ((), ()))
    for k in range(blocks):
        q = jnp.concatenate([g[i, k].reshape(cols, depth) for i in range(wide)], axis=1)
        plain = lax.dot_general(x[...], q, last, preferred_element_type=F32)
        rot_ref[k] = plain.astype(BF16)
        mapped = lax.dot_general(hx[...], q, last, preferred_element_type=F32)
        cor_ref[k] = ((mapped - plain * ritz_ref[k : k + 1, :]) * inv[k]).astype(BF16)

    first = (((0,), (0,)), ((), ()))
    chip = w // 2
    core = w % 2
    block_shape = p16.shape[3:]
    order = (3, 1, 2, 0)
    for j in order:
        m = flip(chip, j)
        xc = x[:, pl.ds(pl.multiple_of(m * (2 * depth), 2 * depth), 2 * depth)]
        for k in range(blocks):
            part = lax.dot_general(cor_ref[k], xc, first, preferred_element_type=F32)
            for h in range(2):
                half = part[:, h * depth : (h + 1) * depth].reshape(block_shape)
                p32[j, h, k] = half
                p16[j, h, k] = half.astype(BF16)
        push(p16.at[j, 1 - core], r1.at[j], s1.at[j], t1.at[j], wide_to(CORE))

    lead = (XBIT, YBIT)
    for j in order:
        arrived(r1.at[j], s1.at[j], t1.at[j], wide_to(CORE))
        for k in range(2):
            total = p32[j, core, k] + r1[j, k].astype(F32)
            if j & (k + 1):
                a16[j, k] = total.astype(BF16)
                at = j ^ (k + 1)
                slot = 0 if at == 0 else 1
                push(a16.at[j, k], r2.at[k, slot], s2.at[k, slot], t2.at[k, slot], wide_to(lead[k]))
            else:
                p32[j, core, k] = total
    for k in range(2):
        j = 2 - k
        arrived(r2.at[k, 1], s2.at[k, 1], t2.at[k, 1], wide_to(lead[k]))
        a16[j, k] = (p32[j, core, k] + r2[k, 1].astype(F32)).astype(BF16)
        push(a16.at[j, k], r3.at[k], s3.at[k], t3.at[k], wide_to(lead[1 - k]))
    for k in range(2):
        arrived(r2.at[k, 0], s2.at[k, 0], t2.at[k, 0], wide_to(lead[k]))
        arrived(r3.at[k], s3.at[k], t3.at[k], wide_to(lead[1 - k]))
        total = p32[0, core, k] + r2[k, 0].astype(F32) + r3[k].astype(F32)
        f32s[k] = total
        f16[k] = total.astype(BF16)
    for d in range(1, narrow):
        push(f16.at[:, flip(n, d)], r4.at[d], s4.at[d], t4.at[d], narrow_to(d))
    out = f32s[:, n]
    for d in range(1, narrow):
        arrived(r4.at[d], s4.at[d], t4.at[d], narrow_to(d))
        out = out + r4[d].astype(F32)
    mar_ref[...] = out * factor
    for copy in sends:
        copy.wait_send()


def fused(wide, narrow, states, applied, rotation, ritz, potential):
    rows, nst = states.shape
    blocks, depth, part = rotation.shape
    cols = part * narrow
    factor = 1.0 / math.sqrt(rows * wide * narrow)
    dma = pltpu.SemaphoreType.DMA
    vmem = pl.BlockSpec(memory_space=pltpu.VMEM)
    hbm = pl.BlockSpec(memory_space=pltpu.HBM)
    tile = (narrow, part, depth)
    chips = wide // 2
    rot, cor, mar = pl.pallas_call(
        functools.partial(fused_kernel, factor, narrow),
        out_shape=(
            jax.ShapeDtypeStruct((blocks, rows, cols), BF16),
            jax.ShapeDtypeStruct((blocks, rows, cols), BF16),
            jax.ShapeDtypeStruct((blocks, part, depth), F32),
        ),
        in_specs=[vmem, vmem, vmem, hbm, hbm],
        out_specs=(vmem, vmem, vmem),
        scratch_shapes=[
            pltpu.VMEM((rows, nst), BF16),
            pltpu.VMEM((rows, nst), BF16),
            pltpu.VMEM((wide, blocks) + tile, BF16),
            pltpu.VMEM((blocks, rows, cols), F32),
            pltpu.VMEM((chips, 2, blocks) + tile, F32),
            pltpu.VMEM((chips, 2, blocks) + tile, BF16),
            pltpu.VMEM((chips, blocks) + tile, BF16),
            pltpu.VMEM((chips, blocks) + tile, BF16),
            pltpu.VMEM((blocks, 2) + tile, BF16),
            pltpu.VMEM((blocks,) + tile, BF16),
            pltpu.VMEM((blocks,) + tile, F32),
            pltpu.VMEM((blocks,) + tile, BF16),
            pltpu.VMEM((narrow, blocks, part, depth), BF16),
            dma((2,)),
            dma((narrow,)), dma((narrow,)),
            dma((3, narrow)), dma((3, narrow)),
            dma((2, narrow)), dma((2, narrow)),
            dma((4, narrow)), dma((4, narrow)),
            dma((chips,)), dma((chips,)),
            dma((2, 2)), dma((2, 2)),
            dma((2,)), dma((2,)),
            dma((narrow,)), dma((narrow,)),
        ],
        compiler_params=pltpu.CompilerParams(
            collective_id=0, has_side_effects=True, vmem_limit_bytes=40 * 1024 * 1024),
    )(jnp.swapaxes(rotation, 1, 2), ritz, potential.reshape(1, rows), states, applied)
    return (
        jnp.swapaxes(rot, 0, 1),
        jnp.swapaxes(cor, 0, 1),
        jnp.swapaxes(mar, 1, 2),
    )


def plain_path(states, applied, rotation, ritz, potential):
    row_count = states.shape[0]
    total_rows = row_count * lax.axis_size("wide") * lax.axis_size("narrow")
    factor = 1.0 / math.sqrt(total_rows)
    contract = (((0,), (0,)), ((), ()))
    rotated_list = []
    correction_list = []
    margin_list = []
    for window in range(rotation.shape[0]):
        q_local = rotation[window]
        q_tall = lax.all_gather(q_local, "wide", axis=0, tiled=True)
        q_full = lax.all_gather(q_tall, "narrow", axis=1, tiled=True)
        plain = jnp.dot(states, q_full, preferred_element_type=F32)
        mapped = jnp.dot(applied, q_full, preferred_element_type=F32)
        eigen_values = ritz[window]
        residual = mapped - plain * eigen_values[None, :]
        fixed = (residual / (potential[:, None] + eigen_values[None, :])).astype(BF16)
        partial_value = lax.psum_scatter(
            lax.dot_general(states, fixed, contract, preferred_element_type=F32).astype(BF16),
            "wide",
            scatter_dimension=0,
            tiled=True,
        )
        summed = lax.psum_scatter(partial_value, "narrow", scatter_dimension=1, tiled=True).astype(F32)
        rotated_list.append(plain.astype(BF16))
        correction_list.append(fixed)
        margin_list.append(summed * factor)
    return (
        jnp.stack(rotated_list, axis=1),
        jnp.stack(correction_list, axis=1),
        jnp.stack(margin_list, axis=0),
    )


def solution(mesh):
    wide, narrow = mesh.shape["wide"], mesh.shape["narrow"]

    def per_device(states, applied, rotation, ritz, potential):
        blocks, depth, part = rotation.shape
        fits = (
            wide == 1 << 3 and narrow & (narrow - 1) == 0 and blocks == 2
            and depth % 128 == 0 and part % 16 == 0 and states.shape[0] % 128 == 0
        )
        if fits:
            return fused(wide, narrow, states, applied, rotation, ritz, potential)
        return plain_path(states, applied, rotation, ritz, potential)

    placed = (
        P(("wide", "narrow"), None),
        P(("wide", "narrow"), None),
        P(None, "wide", "narrow"),
        P(),
        P(("wide", "narrow")),
    )
    return jax.shard_map(
        per_device,
        mesh=mesh,
        in_specs=placed,
        out_specs=(
            P(("wide", "narrow"), None, None),
            P(("wide", "narrow"), None, None),
            P(None, "wide", "narrow"),
        ),
        check_vma=False,
    )
```

```python
import functools
import math

import jax
import jax.numpy as jnp
from jax import lax
from jax.experimental import pallas as pl
from jax.experimental.pallas import tpu as pltpu
from jax.sharding import PartitionSpec as P

F32 = jnp.float32
BF16 = jnp.bfloat16
CORE, XBIT, YBIT = 1, 2, 4


def flip(index, mask):
    out = index
    bit = 1
    while bit <= mask:
        if mask & bit:
            out = out + bit * (1 - 2 * ((index // bit) % 2))
        bit *= 2
    return out


def fused_kernel(
    factor, narrow,
    q_hbm, ritz_hbm, pot_hbm, x_hbm, hx_hbm,
    rot_hbm, cor_hbm, mar_ref,
    rot_ref, cor_ref, rot_out, cor_out, out_sem, q_ref, ritz_ref, pot_ref, x, hx, g, inv, p32, p16, a16, r1, r2, f16, r4,
    in_sem, zs, zr, gs, gr, cs, cr, s1, t1, s2, t2, s4, t4,
):
    w = lax.axis_index("wide")
    n = lax.axis_index("narrow")
    blocks = q_ref.shape[0]
    loads = [
        pltpu.make_async_copy(src, dst, in_sem.at[i])
        for i, (src, dst) in enumerate(
            ((q_hbm, q_ref), (ritz_hbm, ritz_ref), (pot_hbm, pot_ref), (x_hbm, x), (hx_hbm, hx)))
    ]
    for load in loads:
        load.start()
    wide_to = lambda mask: {"wide": flip(w, mask)}
    narrow_to = lambda d: {"narrow": flip(n, d)}
    sends = []

    def push(src, dst, send, recv, to):
        copy = pltpu.make_async_remote_copy(
            src_ref=src, dst_ref=dst, send_sem=send, recv_sem=recv,
            device_id=to, device_id_type=pl.DeviceIdType.MESH)
        copy.start()
        sends.append(copy)

    def arrived(dst, send, recv, to):
        pltpu.make_async_remote_copy(
            src_ref=dst, dst_ref=dst, send_sem=send, recv_sem=recv,
            device_id=to, device_id_type=pl.DeviceIdType.MESH).wait_recv()

    barrier = pltpu.get_barrier_semaphore()
    peers = [wide_to(m) for m in (CORE, XBIT, YBIT, XBIT | YBIT)] + [narrow_to(d) for d in range(1, narrow)]
    for peer in peers:
        pl.semaphore_signal(barrier, inc=1, device_id=peer, device_id_type=pl.DeviceIdType.MESH)
    loads[0].wait()
    pl.semaphore_wait(barrier, len(peers))

    near = (XBIT | YBIT, XBIT, YBIT)
    for d in range(narrow - 1, 0, -1):
        push(q_ref, g.at[w, :, n], zs.at[d], zr.at[d], narrow_to(d))
    for i, m in enumerate(near + (CORE,)):
        push(q_ref, g.at[w, :, n], gs.at[i, 0], gr.at[i, 0], wide_to(m))
    g[w, :, n] = q_ref[...]
    for d in range(1, narrow):
        nd = flip(n, d)
        arrived(g.at[w, :, nd], zs.at[d], zr.at[d], narrow_to(d))
        for i, m in enumerate(near + (CORE,)):
            push(g.at[w, :, nd], g.at[w, :, nd], gs.at[i, d], gr.at[i, d], wide_to(m))

    loads[1].wait()
    loads[2].wait()
    pot_col = jnp.transpose(jnp.broadcast_to(pot_ref[...], (128, pot_ref.shape[1])))[:, :1]
    for k in range(blocks):
        inv[k] = 1.0 / (pot_col + ritz_ref[k : k + 1, :])

    for d in range(narrow):
        nd = flip(n, d)
        for i, m in enumerate(near):
            wm = flip(w, m)
            arrived(g.at[wm, :, nd], gs.at[i, d], gr.at[i, d], wide_to(m))
            push(g.at[wm, :, nd], g.at[wm, :, nd], cs.at[i, d], cr.at[i, d], wide_to(CORE))
    for d in range(narrow):
        nd = flip(n, d)
        arrived(g.at[flip(w, CORE), :, nd], gs.at[3, d], gr.at[3, d], wide_to(CORE))
        for i, m in enumerate(near):
            arrived(g.at[flip(w, m | CORE), :, nd], cs.at[i, d], cr.at[i, d], wide_to(CORE))
    loads[3].wait()
    loads[4].wait()

    wide = g.shape[0]
    cols = g.shape[2] * g.shape[3]
    depth = g.shape[4]
    last = (((1,), (1,)), ((), ()))
    for k in range(blocks):
        q = jnp.concatenate([g[i, k].reshape(cols, depth) for i in range(wide)], axis=1)
        plain = lax.dot_general(x[...], q, last, preferred_element_type=F32)
        rot_ref[k] = plain
        mapped = lax.dot_general(hx[...], q, last, preferred_element_type=F32)
        cor_ref[k] = ((mapped - plain * ritz_ref[k : k + 1, :]) * inv[k]).astype(BF16)

    first = (((0,), (0,)), ((), ()))
    chips = wide // 2
    chip = w // 2
    core = w % 2
    for m in range(chips):
        xc = x[:, 2 * m * depth : 2 * (m + 1) * depth]
        for k in range(blocks):
            part = lax.dot_general(cor_ref[k], xc, first, preferred_element_type=F32)
            for h in range(2):
                half = part[:, h * depth : (h + 1) * depth].reshape(g.shape[2:])
                p32[h, :, m, k] = half
                p16[h, :, m, k] = half.astype(BF16)
    away = range(narrow - 1, -1, -1)
    for d in away:
        push(p16.at[1 - core, flip(n, d)], r1.at[d], s1.at[d], t1.at[d], wide_to(CORE))
    for d in away:
        nd = flip(n, d)
        arrived(r1.at[d], s1.at[d], t1.at[d], wide_to(CORE))
        for i, m in enumerate(near):
            j = flip(chip, m // 2)
            a16[d, i] = (p32[core, nd, j] + r1[d, j].astype(F32)).astype(BF16)
            push(a16.at[d, i], r2.at[d, i], s2.at[d, i], t2.at[d, i], wide_to(m))
    outs = []
    for i, (src, dst, dst_hbm) in enumerate(((rot_ref, rot_out, rot_hbm), (cor_ref, cor_out, cor_hbm))):
        dst[...] = jnp.stack([src[k].astype(F32) for k in range(blocks)], axis=1).astype(BF16)
        out = pltpu.make_async_copy(dst, dst_hbm, out_sem.at[i])
        out.start()
        outs.append(out)
    for d in away:
        total = p32[core, flip(n, d), chip] + r1[d, chip].astype(F32)
        for i, m in enumerate(near):
            arrived(r2.at[d, i], s2.at[d, i], t2.at[d, i], wide_to(m))
            total = total + r2[d, i].astype(F32)
        if d > 0:
            f16[d] = total.astype(BF16)
            push(f16.at[d], r4.at[d], s4.at[d], t4.at[d], narrow_to(d))
    for d in away[:-1]:
        arrived(r4.at[d], s4.at[d], t4.at[d], narrow_to(d))
        total = total + r4[d].astype(F32)
    mar_ref[...] = total * factor
    for out in outs:
        out.wait()
    for copy in sends:
        copy.wait_send()


def hand_over_kernel(cuts, *refs):
    count = len(cuts)
    sources, targets, held = refs[:count], refs[count : 2 * count], refs[2 * count : 3 * count]
    in_sem, out_sem = refs[3 * count :]
    pieces = []
    for a, pieces_of in enumerate(cuts):
        size = sources[a].shape[0] // pieces_of
        pieces += [(a, pl.ds(i * size, size)) for i in range(pieces_of)]
    reads = [
        pltpu.make_async_copy(sources[a].at[cut], held[a].at[cut], in_sem.at[i])
        for i, (a, cut) in enumerate(pieces)
    ]
    writes = [
        pltpu.make_async_copy(held[a].at[cut], targets[a].at[cut], out_sem.at[i])
        for i, (a, cut) in enumerate(pieces)
    ]
    for read in reads:
        read.start()
    for read, write in zip(reads, writes):
        read.wait()
        write.start()
    for write in writes:
        write.wait()


def hand_over(arrays, cuts):
    hbm = pl.BlockSpec(memory_space=pltpu.HBM)
    return pl.pallas_call(
        functools.partial(hand_over_kernel, cuts),
        out_shape=tuple(jax.ShapeDtypeStruct(a.shape, a.dtype) for a in arrays),
        in_specs=[hbm] * len(arrays),
        out_specs=(hbm,) * len(arrays),
        scratch_shapes=[pltpu.VMEM(a.shape, a.dtype) for a in arrays]
        + [pltpu.SemaphoreType.DMA((sum(cuts),))] * 2,
        compiler_params=pltpu.CompilerParams(vmem_limit_bytes=60 * 1024 * 1024),
    )(*arrays)


def fused(wide, narrow, states, applied, rotation, ritz, potential):
    rows, nst = states.shape
    blocks, depth, part = rotation.shape
    cols = part * narrow
    factor = 1.0 / math.sqrt(rows * wide * narrow)
    dma = pltpu.SemaphoreType.DMA
    vmem = pl.BlockSpec(memory_space=pltpu.VMEM)
    hbm = pl.BlockSpec(memory_space=pltpu.HBM)
    tile = (narrow, part, depth)
    tile_in = (blocks, part, depth)
    chips = wide // 2
    rot, cor, mar = pl.pallas_call(
        functools.partial(fused_kernel, factor, narrow),
        out_shape=(
            jax.ShapeDtypeStruct((rows, blocks, cols), BF16),
            jax.ShapeDtypeStruct((rows, blocks, cols), BF16),
            jax.ShapeDtypeStruct((blocks, part, depth), F32),
        ),
        in_specs=[hbm] * 5,
        out_specs=(hbm, hbm, vmem),
        scratch_shapes=[
            pltpu.VMEM((blocks, rows, cols), F32),
            pltpu.VMEM((blocks, rows, cols), BF16),
            pltpu.VMEM((rows, blocks, cols), BF16),
            pltpu.VMEM((rows, blocks, cols), BF16),
            dma((2,)),
            pltpu.VMEM(tile_in, BF16),
            pltpu.VMEM(ritz.shape, F32),
            pltpu.VMEM((1, rows), F32),
            pltpu.VMEM((rows, nst), BF16),
            pltpu.VMEM((rows, nst), BF16),
            pltpu.VMEM((wide, blocks) + tile, BF16),
            pltpu.VMEM((blocks, rows, cols), F32),
            pltpu.VMEM((2, narrow, chips) + tile_in, F32),
            pltpu.VMEM((2, narrow, chips) + tile_in, BF16),
            pltpu.VMEM((narrow, 3) + tile_in, BF16),
            pltpu.VMEM((narrow, chips) + tile_in, BF16),
            pltpu.VMEM((narrow, 3) + tile_in, BF16),
            pltpu.VMEM((narrow,) + tile_in, BF16),
            pltpu.VMEM((narrow,) + tile_in, BF16),
            dma((5,)),
            dma((narrow,)), dma((narrow,)),
            dma((4, narrow)), dma((4, narrow)),
            dma((3, narrow)), dma((3, narrow)),
            dma((narrow,)), dma((narrow,)),
            dma((narrow, 3)), dma((narrow, 3)),
            dma((narrow,)), dma((narrow,)),
        ],
        compiler_params=pltpu.CompilerParams(
            collective_id=0, has_side_effects=True, vmem_limit_bytes=60 * 1024 * 1024),
    )(jnp.swapaxes(rotation, 1, 2), ritz, potential.reshape(1, rows), states, applied)
    rot, cor, mar = hand_over((rot, cor, mar), (2, 2, 1))
    return (
        rot,
        cor,
        jnp.swapaxes(mar, 1, 2),
    )


def plain_path(states, applied, rotation, ritz, potential):
    row_count = states.shape[0]
    total_rows = row_count * lax.axis_size("wide") * lax.axis_size("narrow")
    factor = 1.0 / math.sqrt(total_rows)
    contract = (((0,), (0,)), ((), ()))
    rotated_list = []
    correction_list = []
    margin_list = []
    for window in range(rotation.shape[0]):
        q_local = rotation[window]
        q_tall = lax.all_gather(q_local, "wide", axis=0, tiled=True)
        q_full = lax.all_gather(q_tall, "narrow", axis=1, tiled=True)
        plain = jnp.dot(states, q_full, preferred_element_type=F32)
        mapped = jnp.dot(applied, q_full, preferred_element_type=F32)
        eigen_values = ritz[window]
        residual = mapped - plain * eigen_values[None, :]
        fixed = (residual / (potential[:, None] + eigen_values[None, :])).astype(BF16)
        partial_value = lax.psum_scatter(
            lax.dot_general(states, fixed, contract, preferred_element_type=F32).astype(BF16),
            "wide",
            scatter_dimension=0,
            tiled=True,
        )
        summed = lax.psum_scatter(partial_value, "narrow", scatter_dimension=1, tiled=True).astype(F32)
        rotated_list.append(plain.astype(BF16))
        correction_list.append(fixed)
        margin_list.append(summed * factor)
    return (
        jnp.stack(rotated_list, axis=1),
        jnp.stack(correction_list, axis=1),
        jnp.stack(margin_list, axis=0),
    )


def solution(mesh):
    wide, narrow = mesh.shape["wide"], mesh.shape["narrow"]

    def per_device(states, applied, rotation, ritz, potential):
        blocks, depth, part = rotation.shape
        fits = (
            wide == 1 << 3 and narrow & (narrow - 1) == 0 and blocks == 2
            and depth % 128 == 0 and part % 16 == 0 and states.shape[0] % 128 == 0
        )
        if fits:
            return fused(wide, narrow, states, applied, rotation, ritz, potential)
        return plain_path(states, applied, rotation, ritz, potential)

    placed = (
        P(("wide", "narrow"), None),
        P(("wide", "narrow"), None),
        P(None, "wide", "narrow"),
        P(),
        P(("wide", "narrow")),
    )
    return jax.shard_map(
        per_device,
        mesh=mesh,
        in_specs=placed,
        out_specs=(
            P(("wide", "narrow"), None, None),
            P(("wide", "narrow"), None, None),
            P(None, "wide", "narrow"),
        ),
        check_vma=False,
    )
```

```python
import functools
import math

import jax
import jax.numpy as jnp
from jax import lax
from jax.experimental import pallas as pl
from jax.experimental.pallas import tpu as pltpu
from jax.sharding import PartitionSpec as P

F32 = jnp.float32
BF16 = jnp.bfloat16
CORE, XBIT, YBIT = 1, 2, 4


def flip(index, mask):
    out = index
    bit = 1
    while bit <= mask:
        if mask & bit:
            out = out + bit * (1 - 2 * ((index // bit) % 2))
        bit *= 2
    return out


def fused_kernel(
    factor, narrow,
    q_hbm, ritz_hbm, pot_hbm, x_hbm, hx_hbm,
    rot_hbm, cor_hbm, mar_ref,
    rot_ref, cor_ref, rot_out, cor_out, out_sem, q_ref, ritz_ref, pot_ref, x, hx, g, inv, p32, p16, a16, r1, r2, f16, r4,
    in_sem, zs, zr, gs, gr, cs, cr, s1, t1, s2, t2, s4, t4,
):
    w = lax.axis_index("wide")
    n = lax.axis_index("narrow")
    blocks = q_ref.shape[0]
    loads = [
        pltpu.make_async_copy(src, dst, in_sem.at[i])
        for i, (src, dst) in enumerate(
            ((q_hbm, q_ref), (ritz_hbm, ritz_ref), (pot_hbm, pot_ref), (x_hbm, x), (hx_hbm, hx)))
    ]
    for load in loads:
        load.start()
    wide_to = lambda mask: {"wide": flip(w, mask)}
    narrow_to = lambda d: {"narrow": flip(n, d)}
    sends = []

    def push(src, dst, send, recv, to):
        copy = pltpu.make_async_remote_copy(
            src_ref=src, dst_ref=dst, send_sem=send, recv_sem=recv,
            device_id=to, device_id_type=pl.DeviceIdType.MESH)
        copy.start()
        sends.append(copy)

    def arrived(dst, send, recv, to):
        pltpu.make_async_remote_copy(
            src_ref=dst, dst_ref=dst, send_sem=send, recv_sem=recv,
            device_id=to, device_id_type=pl.DeviceIdType.MESH).wait_recv()

    barrier = pltpu.get_barrier_semaphore()
    peers = [wide_to(m) for m in (CORE, XBIT, YBIT, XBIT | YBIT)] + [narrow_to(d) for d in range(1, narrow)]
    for peer in peers:
        pl.semaphore_signal(barrier, inc=1, device_id=peer, device_id_type=pl.DeviceIdType.MESH)
    loads[0].wait()
    pl.semaphore_wait(barrier, len(peers))

    near = (XBIT | YBIT, XBIT, YBIT)
    for k in range(blocks):
        for d in range(narrow - 1, 0, -1):
            push(q_ref.at[k], g.at[k, w, n], zs.at[k, d], zr.at[k, d], narrow_to(d))
        for i, m in enumerate(near + (CORE,)):
            push(q_ref.at[k], g.at[k, w, n], gs.at[k, i, 0], gr.at[k, i, 0], wide_to(m))
        g[k, w, n] = q_ref[k]
    for k in range(blocks):
        for d in range(1, narrow):
            own = g.at[k, w, flip(n, d)]
            arrived(own, zs.at[k, d], zr.at[k, d], narrow_to(d))
            for i, m in enumerate(near + (CORE,)):
                push(own, own, gs.at[k, i, d], gr.at[k, i, d], wide_to(m))

    loads[1].wait()
    loads[2].wait()
    pot_col = jnp.transpose(jnp.broadcast_to(pot_ref[...], (128, pot_ref.shape[1])))[:, :1]
    for k in range(blocks):
        inv[k] = 1.0 / (pot_col + ritz_ref[k : k + 1, :])

    def pass_on(k):
        for d in range(narrow):
            for i, m in enumerate(near):
                block = g.at[k, flip(w, m), flip(n, d)]
                arrived(block, gs.at[k, i, d], gr.at[k, i, d], wide_to(m))
                push(block, block, cs.at[k, i, d], cr.at[k, i, d], wide_to(CORE))

    def gathered(k):
        for d in range(narrow):
            nd = flip(n, d)
            arrived(g.at[k, flip(w, CORE), nd], gs.at[k, 3, d], gr.at[k, 3, d], wide_to(CORE))
            for i, m in enumerate(near):
                arrived(g.at[k, flip(w, m | CORE), nd], cs.at[k, i, d], cr.at[k, i, d], wide_to(CORE))

    wide = g.shape[1]
    cols = g.shape[2] * g.shape[3]
    depth = g.shape[4]
    chips = wide // 2
    chip = w // 2
    core = w % 2
    last = (((1,), (1,)), ((), ()))
    first = (((0,), (0,)), ((), ()))
    away = range(narrow - 1, -1, -1)

    def products(k):
        q = jnp.concatenate([g[k, i].reshape(cols, depth) for i in range(wide)], axis=1)
        plain = lax.dot_general(x[...], q, last, preferred_element_type=F32)
        rot_ref[k] = plain
        mapped = lax.dot_general(hx[...], q, last, preferred_element_type=F32)
        cor_ref[k] = ((mapped - plain * ritz_ref[k : k + 1, :]) * inv[k]).astype(BF16)

    def partials(k):
        for m in range(chips):
            xc = x[:, 2 * m * depth : 2 * (m + 1) * depth]
            part = lax.dot_general(cor_ref[k], xc, first, preferred_element_type=F32)
            for h in range(2):
                half = part[:, h * depth : (h + 1) * depth].reshape(g.shape[2:])
                p32[k, h, :, m] = half
                p16[k, h, :, m] = half.astype(BF16)
        for d in away:
            push(p16.at[k, 1 - core, flip(n, d)], r1.at[k, d], s1.at[k, d], t1.at[k, d], wide_to(CORE))

    def spread(k):
        for d in away:
            nd = flip(n, d)
            arrived(r1.at[k, d], s1.at[k, d], t1.at[k, d], wide_to(CORE))
            for i, m in enumerate(near):
                j = flip(chip, m // 2)
                a16[k, d, i] = (p32[k, core, nd, j] + r1[k, d, j].astype(F32)).astype(BF16)
                push(a16.at[k, d, i], r2.at[k, d, i], s2.at[k, d, i], t2.at[k, d, i], wide_to(m))

    pass_on(0)
    gathered(0)
    loads[3].wait()
    loads[4].wait()
    products(0)
    for k in range(1, blocks):
        pass_on(k)
        partials(k - 1)
        gathered(k)
        products(k)
        spread(k - 1)
    partials(blocks - 1)
    spread(blocks - 1)

    outs = []
    for i, (src, dst, dst_hbm) in enumerate(((rot_ref, rot_out, rot_hbm), (cor_ref, cor_out, cor_hbm))):
        dst[...] = jnp.stack([src[k].astype(F32) for k in range(blocks)], axis=1).astype(BF16)
        out = pltpu.make_async_copy(dst, dst_hbm, out_sem.at[i])
        out.start()
        outs.append(out)
    for k in range(blocks):
        for d in away:
            total = p32[k, core, flip(n, d), chip] + r1[k, d, chip].astype(F32)
            for i, m in enumerate(near):
                arrived(r2.at[k, d, i], s2.at[k, d, i], t2.at[k, d, i], wide_to(m))
                total = total + r2[k, d, i].astype(F32)
            if d > 0:
                f16[k, d] = total.astype(BF16)
                push(f16.at[k, d], r4.at[k, d], s4.at[k, d], t4.at[k, d], narrow_to(d))
        mar_ref[k] = total
    for k in range(blocks):
        total = mar_ref[k]
        for d in away[:-1]:
            arrived(r4.at[k, d], s4.at[k, d], t4.at[k, d], narrow_to(d))
            total = total + r4[k, d].astype(F32)
        mar_ref[k] = total * factor
    for out in outs:
        out.wait()
    for copy in sends:
        copy.wait_send()


def hand_over_kernel(cuts, *refs):
    count = len(cuts)
    sources, targets, held = refs[:count], refs[count : 2 * count], refs[2 * count : 3 * count]
    in_sem, out_sem = refs[3 * count :]
    pieces = []
    for a, pieces_of in enumerate(cuts):
        size = sources[a].shape[0] // pieces_of
        pieces += [(a, pl.ds(i * size, size)) for i in range(pieces_of)]
    reads = [
        pltpu.make_async_copy(sources[a].at[cut], held[a].at[cut], in_sem.at[i])
        for i, (a, cut) in enumerate(pieces)
    ]
    writes = [
        pltpu.make_async_copy(held[a].at[cut], targets[a].at[cut], out_sem.at[i])
        for i, (a, cut) in enumerate(pieces)
    ]
    for read in reads:
        read.start()
    for read, write in zip(reads, writes):
        read.wait()
        write.start()
    for write in writes:
        write.wait()


def hand_over(arrays, cuts):
    hbm = pl.BlockSpec(memory_space=pltpu.HBM)
    return pl.pallas_call(
        functools.partial(hand_over_kernel, cuts),
        out_shape=tuple(jax.ShapeDtypeStruct(a.shape, a.dtype) for a in arrays),
        in_specs=[hbm] * len(arrays),
        out_specs=(hbm,) * len(arrays),
        scratch_shapes=[pltpu.VMEM(a.shape, a.dtype) for a in arrays]
        + [pltpu.SemaphoreType.DMA((sum(cuts),))] * 2,
        compiler_params=pltpu.CompilerParams(vmem_limit_bytes=60 * 1024 * 1024),
    )(*arrays)


def fused(wide, narrow, states, applied, rotation, ritz, potential):
    rows, nst = states.shape
    blocks, depth, part = rotation.shape
    cols = part * narrow
    factor = 1.0 / math.sqrt(rows * wide * narrow)
    dma = pltpu.SemaphoreType.DMA
    vmem = pl.BlockSpec(memory_space=pltpu.VMEM)
    hbm = pl.BlockSpec(memory_space=pltpu.HBM)
    unit = (part, depth)
    tile_in = (blocks, part, depth)
    chips = wide // 2
    rot, cor, mar = pl.pallas_call(
        functools.partial(fused_kernel, factor, narrow),
        out_shape=(
            jax.ShapeDtypeStruct((rows, blocks, cols), BF16),
            jax.ShapeDtypeStruct((rows, blocks, cols), BF16),
            jax.ShapeDtypeStruct((blocks, part, depth), F32),
        ),
        in_specs=[hbm] * 5,
        out_specs=(hbm, hbm, vmem),
        scratch_shapes=[
            pltpu.VMEM((blocks, rows, cols), F32),
            pltpu.VMEM((blocks, rows, cols), BF16),
            pltpu.VMEM((rows, blocks, cols), BF16),
            pltpu.VMEM((rows, blocks, cols), BF16),
            dma((2,)),
            pltpu.VMEM(tile_in, BF16),
            pltpu.VMEM(ritz.shape, F32),
            pltpu.VMEM((1, rows), F32),
            pltpu.VMEM((rows, nst), BF16),
            pltpu.VMEM((rows, nst), BF16),
            pltpu.VMEM((blocks, wide, narrow) + unit, BF16),
            pltpu.VMEM((blocks, rows, cols), F32),
            pltpu.VMEM((blocks, 2, narrow, chips) + unit, F32),
            pltpu.VMEM((blocks, 2, narrow, chips) + unit, BF16),
            pltpu.VMEM((blocks, narrow, 3) + unit, BF16),
            pltpu.VMEM((blocks, narrow, chips) + unit, BF16),
            pltpu.VMEM((blocks, narrow, 3) + unit, BF16),
            pltpu.VMEM((blocks, narrow) + unit, BF16),
            pltpu.VMEM((blocks, narrow) + unit, BF16),
            dma((5,)),
            dma((blocks, narrow)), dma((blocks, narrow)),
            dma((blocks, 4, narrow)), dma((blocks, 4, narrow)),
            dma((blocks, 3, narrow)), dma((blocks, 3, narrow)),
            dma((blocks, narrow)), dma((blocks, narrow)),
            dma((blocks, narrow, 3)), dma((blocks, narrow, 3)),
            dma((blocks, narrow)), dma((blocks, narrow)),
        ],
        compiler_params=pltpu.CompilerParams(
            collective_id=0, has_side_effects=True, vmem_limit_bytes=60 * 1024 * 1024),
    )(jnp.swapaxes(rotation, 1, 2), ritz, potential.reshape(1, rows), states, applied)
    rot, cor, mar = hand_over((rot, cor, mar), (2, 2, 1))
    return (
        rot,
        cor,
        jnp.swapaxes(mar, 1, 2),
    )


def plain_path(states, applied, rotation, ritz, potential):
    row_count = states.shape[0]
    total_rows = row_count * lax.axis_size("wide") * lax.axis_size("narrow")
    factor = 1.0 / math.sqrt(total_rows)
    contract = (((0,), (0,)), ((), ()))
    rotated_list = []
    correction_list = []
    margin_list = []
    for window in range(rotation.shape[0]):
        q_local = rotation[window]
        q_tall = lax.all_gather(q_local, "wide", axis=0, tiled=True)
        q_full = lax.all_gather(q_tall, "narrow", axis=1, tiled=True)
        plain = jnp.dot(states, q_full, preferred_element_type=F32)
        mapped = jnp.dot(applied, q_full, preferred_element_type=F32)
        eigen_values = ritz[window]
        residual = mapped - plain * eigen_values[None, :]
        fixed = (residual / (potential[:, None] + eigen_values[None, :])).astype(BF16)
        partial_value = lax.psum_scatter(
            lax.dot_general(states, fixed, contract, preferred_element_type=F32).astype(BF16),
            "wide",
            scatter_dimension=0,
            tiled=True,
        )
        summed = lax.psum_scatter(partial_value, "narrow", scatter_dimension=1, tiled=True).astype(F32)
        rotated_list.append(plain.astype(BF16))
        correction_list.append(fixed)
        margin_list.append(summed * factor)
    return (
        jnp.stack(rotated_list, axis=1),
        jnp.stack(correction_list, axis=1),
        jnp.stack(margin_list, axis=0),
    )


def solution(mesh):
    wide, narrow = mesh.shape["wide"], mesh.shape["narrow"]

    def per_device(states, applied, rotation, ritz, potential):
        blocks, depth, part = rotation.shape
        fits = (
            wide == 1 << 3 and narrow & (narrow - 1) == 0 and blocks == 2
            and depth % 128 == 0 and part % 16 == 0 and states.shape[0] % 128 == 0
        )
        if fits:
            return fused(wide, narrow, states, applied, rotation, ritz, potential)
        return plain_path(states, applied, rotation, ritz, potential)

    placed = (
        P(("wide", "narrow"), None),
        P(("wide", "narrow"), None),
        P(None, "wide", "narrow"),
        P(),
        P(("wide", "narrow")),
    )
    return jax.shard_map(
        per_device,
        mesh=mesh,
        in_specs=placed,
        out_specs=(
            P(("wide", "narrow"), None, None),
            P(("wide", "narrow"), None, None),
            P(None, "wide", "narrow"),
        ),
        check_vma=False,
    )
```
